32 devices in a mesh: grp: 2 (over x), sp: 16 (over z, y, core).
Axes of the slice: x: 2, y: 2, z: 4, core: 2. Of those that a mesh axis runs over, the one named last changes fastest.
Arguments:
- latents: bfloat16 [10240, 64], P(('grp', 'sp')), parts along dimension 0, may hold values from -9 to 9
- row_cell: int32 [10240], P(('grp', 'sp')), parts along dimension 0, may hold values from 0 to 5119, as said below
- w_in: bfloat16 [3, 3, 3, 16, 384], replicated, may hold values from -1 to 1
- b_in: float32 [384], replicated, may hold values from -3 to 3
- gain: float32 [384], replicated, may hold values from 0.1 to 1.9
- w_mid: bfloat16 [3, 3, 3, 384, 384], replicated, may hold values from -0.0625 to 0.0625
- b_mid: float32 [384], replicated, may hold values from -3 to 3
Outputs:
- decoded: bfloat16 [32, 2, 4, 160, 384], P(('grp', 'sp')), parts along dimension 0
The draws below stay inside these ranges and needn't reach their ends.
There are 2 independent parts, one for each index of `grp`. The reference program is written for one: setup_inputs(seed, part) draws one part's arguments, and reference() takes and returns one part's arrays. A program takes and returns all parts, laid end to end along the dimension named above; an argument that names none is the same for every part. Nothing has to cross between parts.
Inputs may be any that keep to these rules, and one draw needn't show every extreme that they name: `row_cell`: every token position appears exactly once. The tile of token (t, i, j) is (t // 2) * 8 + (2 i) // 4. Among the tokens of one device, every tile has 20 tokens, except one tile with 40 and one with none; each tile gets 2 * 20 tokens from exactly one device. Order within a device is arbitrary.
All inputs are finite; a program needn't handle non-finite values.
Results may differ from the reference program's by a relative error of at most 0.0051.
Values may be sent and summed in bfloat16 or wider, within the bound.
A program may use at most 128 MiB of HBM per device.

```python
import math
import jax
import jax.numpy as jnp
from jax import lax

C_LAT = 16
C_MID = 384
W = 160
TB = 2
HBANDS = 8
HB = 4
TBLOCKS = 2
TILES = 16
FRAMES = 4
HEIGHT = 32
TOKS = 320
TOKENS = 5120
PAIR = 20


def draw_latents(key, part):
    base = jnp.clip(jax.random.normal(jax.random.fold_in(key, 11), (TOKENS, 4 * C_LAT), jnp.float32), -6.0, 6.0)
    return base.astype(jnp.bfloat16)


def draw_w_in(key, part):
    columns = jnp.exp(jax.random.uniform(jax.random.fold_in(key, 21), (C_MID,), jnp.float32, math.log(0.3), math.log(3.0)))
    entries = jnp.clip(jax.random.normal(jax.random.fold_in(key, 22), (3, 3, 3, C_LAT, C_MID), jnp.float32), -4.0, 4.0)
    return (entries * columns / math.sqrt(27.0 * C_LAT)).astype(jnp.bfloat16)


def draw_row_cell(key, part):
    count = TILES
    keys = jax.random.split(jax.random.fold_in(key, 5), 3)
    favoured = jax.random.permutation(keys[0], count).astype(jnp.int32)
    skipped = jnp.roll(favoured, 1)
    owners = jnp.arange(count, dtype=jnp.int32)
    pair_counts = PAIR + PAIR * ((favoured[:, None] == owners[None, :]).astype(jnp.int32) - (skipped[:, None] == owners[None, :]).astype(jnp.int32))
    upto = jnp.cumsum(pair_counts, axis=0)
    starts = upto - pair_counts
    src_offsets = jnp.cumsum(pair_counts, axis=1) - pair_counts
    within = jnp.arange(TOKS, dtype=jnp.int32)
    source = jnp.sum((upto[:, :, None] <= within[None, None, :]).astype(jnp.int32), axis=0)
    start_of = jnp.take_along_axis(starts.T, source, axis=1)
    offset_of = jnp.take_along_axis(src_offsets.T, source, axis=1)
    place = offset_of + within[None, :] - start_of
    tile_orders = jax.vmap(lambda sub: jax.random.permutation(sub, TOKS))(jax.random.split(keys[1], count)).astype(jnp.int32)
    shuffles = jax.vmap(lambda sub: jax.random.permutation(sub, TOKS))(jax.random.split(keys[2], count)).astype(jnp.int32)
    final_place = source * TOKS + shuffles[source, place]
    half_rows = HB // 2
    half_width = W // 2
    frame_in = tile_orders // (half_rows * half_width)
    row_in = tile_orders // half_width % half_rows
    col_in = tile_orders % half_width
    tile_time = (owners // HBANDS)[:, None]
    tile_band = (owners % HBANDS)[:, None]
    cell = ((tile_time * TB + frame_in) * (HEIGHT // 2) + tile_band * half_rows + row_in) * half_width + col_in
    return jnp.zeros((TOKENS,), jnp.int32).at[final_place.reshape(-1)].set(cell.reshape(-1).astype(jnp.int32))


def bell_draw(rng, extent, width, reach, kind=jnp.bfloat16):
    return jnp.clip(width * jax.random.normal(rng, extent, jnp.float32), -reach, reach).astype(kind)


def setup_inputs(seed: int = 0, part: int = 0) -> dict:
    splits = jax.random.split(jax.random.key(seed), 8)
    own_keys = jax.random.split(jax.random.fold_in(splits[7], part), 8)
    return {
        "latents": draw_latents(jax.random.fold_in(jax.random.fold_in(splits[7], part), 71), part),
        "row_cell": draw_row_cell(jax.random.fold_in(jax.random.fold_in(splits[7], part), 71), part),
        "w_in": draw_w_in(jax.random.fold_in(splits[7], 71), part),
        "b_in": bell_draw(splits[3], (C_MID,), 0.5, 3.0, jnp.float32),
        "gain": jnp.clip(1.0 + 0.18 * jax.random.normal(splits[4], (C_MID,), jnp.float32), 0.1, 1.9),
        "w_mid": bell_draw(splits[5], (3, 3, 3, C_MID, C_MID), (27 * C_MID) ** -0.5, 0.0625),
        "b_mid": bell_draw(splits[6], (C_MID,), 0.5, 3.0, jnp.float32),
    }


def causal_conv(extended, weight):
    frames_out = extended.shape[0] - 2
    rows_out = extended.shape[1] - 2
    tile_width = extended.shape[2]
    channels = extended.shape[3]
    outputs = weight.shape[4]
    padded = jnp.pad(extended, ((0, 0), (0, 0), (1, 1), (0, 0)))
    widened = jnp.concatenate([padded[:, :, offset:offset + tile_width] for offset in range(3)], axis=3)
    accumulated = jnp.zeros((frames_out, rows_out, tile_width, outputs), jnp.float32)
    for tap_time in range(3):
        for tap_row in range(3):
            window = widened[tap_time:tap_time + frames_out, tap_row:tap_row + rows_out]
            kernel = weight[tap_time, tap_row].reshape(3 * channels, outputs)
            accumulated = accumulated + jnp.einsum('thwc,cd->thwd', window.astype(jnp.float32), kernel.astype(jnp.float32))
    return accumulated

def rms_silu(hidden, gain):
    values = hidden.astype(jnp.float32)
    inverse_rms = lax.rsqrt(lax.optimization_barrier(jnp.mean(values * values, axis=-1, keepdims=True)) + 1e-06)
    return jax.nn.silu(values * inverse_rms * gain).astype(jnp.bfloat16)

def reference(latents, row_cell, w_in, b_in, gain, w_mid, b_mid):
    latent_grid = jnp.zeros((TOKENS, 4 * C_LAT), jnp.bfloat16).at[row_cell].set(latents)
    latent_grid = latent_grid.reshape(FRAMES, HEIGHT // 2, W // 2, 2, 2, C_LAT)
    latent_grid = latent_grid.transpose(0, 1, 3, 2, 4, 5).reshape(FRAMES, HEIGHT, W, C_LAT)
    padded_latents = jnp.pad(latent_grid, ((2, 0), (1, 1), (0, 0), (0, 0)))
    hidden = (causal_conv(padded_latents, w_in) + b_in).astype(jnp.bfloat16)
    activated = rms_silu(hidden, gain)
    padded_active = jnp.pad(activated, ((2, 0), (1, 1), (0, 0), (0, 0)))
    mixed = causal_conv(padded_active, w_mid) + b_mid + hidden.astype(jnp.float32)
    decoded = mixed.astype(jnp.bfloat16).reshape(TBLOCKS, TB, HBANDS, HB, W, C_MID)
    decoded = decoded.transpose(0, 2, 1, 3, 4, 5).reshape(TILES, TB, HB, W, C_MID)
    return jnp.roll(decoded, -(2 * HBANDS + HBANDS // 2), axis=0)
```

```python
import functools

import jax
import jax.numpy as jnp
from jax import lax
from jax.experimental import pallas as pl
from jax.experimental.pallas import tpu as pltpu
from jax.sharding import PartitionSpec as P

C_LAT = 16
W = 160
TB = 2
HBANDS = 8
HB = 4
HALF_ROWS = HB // 2
HALF_W = W // 2
OFFSET_TILES = 2 * HBANDS + HBANDS // 2
F32 = jnp.float32
BF16 = jnp.bfloat16


def iota(shape, dim):
    return lax.broadcasted_iota(jnp.int32, shape, dim)


def dot(a, b, dims=((1,), (0,))):
    return lax.dot_general(a, b, (dims, ((), ())), preferred_element_type=F32)


def gather_kernel(n, slots, depth, lat_ref, cell_ref, out_ref, pack, arrived, mine, near,
                  send_a, recv_a, send_b, recv_b):
    me = lax.axis_index("sp")
    toks = lat_ref.shape[0]
    barrier = pltpu.get_barrier_semaphore()
    for delta in range(1, n):
        pl.semaphore_signal(
            barrier, inc=1, device_id={"sp": lax.rem(me + delta, n)},
            device_id_type=pl.DeviceIdType.MESH,
        )
    cell = cell_ref[...].astype(F32)
    line = jnp.floor((cell + 0.5) * (1.0 / HALF_W))
    column = cell - HALF_W * line
    token_rows = HALF_ROWS * HBANDS
    frame = jnp.floor((line + 0.5) * (1.0 / token_rows))
    token_row = line - token_rows * frame
    time_block = jnp.floor((frame + 0.5) * (1.0 / TB))
    band = jnp.floor((token_row + 0.5) * (1.0 / HALF_ROWS))
    place_row = (frame - TB * time_block) * HALF_ROWS + token_row - HALF_ROWS * band
    owner = time_block * HBANDS + band - (OFFSET_TILES % n)
    owner = jnp.where(owner < 0, owner + n, owner)
    hits = owner == iota((n, toks), 0).astype(F32)
    hits = jnp.where(hits, 1.0, 0.0)
    before = jnp.where(iota((toks, toks), 0) < iota((toks, toks), 1), 1.0, 0.0).astype(BF16)
    ranks = dot(hits.astype(BF16), before)
    rank = jnp.sum(ranks * hits, axis=0, keepdims=True)
    target = owner * slots + rank
    picks = jnp.where(target == iota((n * slots, toks), 0).astype(F32), 1.0, 0.0).astype(BF16)
    which = iota((64, toks), 0)
    places = jnp.where(which == 0, place_row + 1.0, jnp.where(which == 1, column, 0.0)).astype(BF16)
    packed = jnp.concatenate(
        [dot(picks, lat_ref[...]), dot(picks, places, ((1,), (1,)))], axis=1
    ).astype(BF16)
    pack[...] = packed.reshape(n, slots, 128)
    arrived[pl.ds(me, 1)] = pack[pl.ds(me, 1)]
    pl.semaphore_wait(barrier, n - 1)
    copies = []
    for delta in range(1, n):
        to = lax.rem(me + delta, n)
        copy = pltpu.make_async_remote_copy(
            src_ref=pack.at[to], dst_ref=arrived.at[me],
            send_sem=send_a.at[delta - 1], recv_sem=recv_a.at[delta - 1],
            device_id={"sp": to}, device_id_type=pl.DeviceIdType.MESH,
        )
        copy.start()
        copies.append(copy)
    for copy in copies:
        copy.wait()
    got = arrived[...].reshape(n * slots, 128)
    got32 = got.astype(F32)
    ident = (got32[:, 64:65] - 1.0) * HALF_W + got32[:, 65:66]
    tokens = got[:, :64]
    odd = (iota((C_LAT, W), 1) & 1) == 1
    half = (iota((1, W), 1) >> 1).astype(F32)
    pieces = []
    for line_in in range(TB * HALF_ROWS):
        spots = jnp.where(ident == half + float(line_in * HALF_W), 1.0, 0.0).astype(BF16)
        grid = dot(tokens, spots, ((0,), (0,)))
        for a in range(2):
            base = a * 2 * C_LAT
            pieces.append(
                jnp.where(odd, grid[base + C_LAT: base + 2 * C_LAT], grid[base: base + C_LAT])
            )
    tile = jnp.concatenate(pieces, axis=0).T.astype(BF16)
    mine[...] = tile

    e = lax.rem(me + OFFSET_TILES, n)
    band_i = lax.rem(e, HBANDS)
    block_i = e // HBANDS
    blocks = n // HBANDS
    for phase in range(3):
        for k in range(depth):
            for side in range(3):
                if k == 0 and side == 1:
                    if phase == 0:
                        out_ref[1] = tile
                    continue
                slot = k * 3 + side
                shift = side - 1
                reader = lax.rem(me + k * HBANDS - shift + n, n)
                send_ok = (block_i + k < blocks)
                if shift == 1:
                    send_ok &= band_i > 0
                if shift == -1:
                    send_ok &= band_i < HBANDS - 1
                recv_ok = block_i >= k
                if shift == 1:
                    recv_ok &= band_i < HBANDS - 1
                if shift == -1:
                    recv_ok &= band_i > 0
                copy = pltpu.make_async_remote_copy(
                    src_ref=mine, dst_ref=near.at[slot],
                    send_sem=send_b.at[slot], recv_sem=recv_b.at[slot],
                    device_id={"sp": reader}, device_id_type=pl.DeviceIdType.MESH,
                )
                if phase == 0:
                    pl.when(send_ok)(copy.start)
                elif phase == 1:
                    def take():
                        copy.wait_recv()
                        out_ref[slot] = near[slot]

                    def blank():
                        out_ref[slot] = jnp.zeros_like(tile)

                    pl.when(recv_ok)(take)
                    pl.when(jnp.logical_not(recv_ok))(blank)
                else:
                    pl.when(send_ok)(copy.wait_send)


def gathered(latents, row_cell):
    n = lax.axis_size("sp")
    toks = latents.shape[0]
    slots = -(-2 * (toks // n) // 16) * 16
    depth = min(3, n // HBANDS)
    return pl.pallas_call(
        functools.partial(gather_kernel, n, slots, depth),
        out_shape=jax.ShapeDtypeStruct((depth * 3, W, 128), BF16),
        in_specs=[pl.BlockSpec(memory_space=pltpu.VMEM)] * 2,
        out_specs=pl.BlockSpec(memory_space=pltpu.VMEM),
        scratch_shapes=[
            pltpu.VMEM((n, slots, 128), BF16),
            pltpu.VMEM((n, slots, 128), BF16),
            pltpu.VMEM((W, 128), BF16),
            pltpu.VMEM((depth * 3, W, 128), BF16),
            pltpu.SemaphoreType.DMA((n - 1,)),
            pltpu.SemaphoreType.DMA((n - 1,)),
            pltpu.SemaphoreType.DMA((depth * 3,)),
            pltpu.SemaphoreType.DMA((depth * 3,)),
        ],
        compiler_params=pltpu.CompilerParams(collective_id=0, has_side_effects=True),
        name="gather_tiles",
    )(latents, row_cell.reshape(1, toks))


def shifted(x):
    where = iota(x.shape, 0)
    right = jnp.where(where == 0, 0.0, pltpu.roll(x, 1, 0))
    left = jnp.where(where == W - 1, 0.0, pltpu.roll(x, W - 1, 0))
    return right, left


def conv_kernel(n, depth, near_ref, w_in_ref, b_in_ref, gain_ref, b_mid_ref, w_mid_ref, out_ref,
                wide, acts, wcat, hidden_ref, acc, sems):
    mid = b_in_ref.shape[1]
    frames = TB + 2
    copies = []
    for index, (half, position, tap) in enumerate(((0, 1, 0), (0, 0, 1), (1, 1, 1), (1, 0, 2))):
        copy = pltpu.make_async_copy(
            w_mid_ref.at[tap], wcat.at[half, :, :, pl.ds(position * mid, mid)], sems.at[index]
        )
        copy.start()
        copies.append(copy)
    e = lax.rem(lax.axis_index("sp") + OFFSET_TILES, n)
    band_i = lax.rem(e, HBANDS)
    block_i = e // HBANDS
    lane = iota((W, 128), 1)
    source = iota((384, 1), 0)
    spread_to = ((source >> 4) & 7) * 48 + (source >> 7) * 16 + (source & 15)
    spread = jnp.where(spread_to == iota((384, 384), 1), 1.0, 0.0).astype(BF16)
    for k in range(3):
        for f in range(TB):
            t = (2 - k) * TB + f
            if k >= depth:
                wide[t] = jnp.zeros((W, 384), BF16)
                continue
            up, own, down = [near_ref[3 * k + side].astype(F32) for side in range(3)]
            x = jnp.where(
                lane < 32, pltpu.roll(up, 96 - 64 * f, 1),
                jnp.where(lane < 96, pltpu.roll(own, (32 - 64 * f) % 128, 1),
                          pltpu.roll(down, (96 - 64 * f) % 128, 1)),
            )
            right, left = shifted(x)
            rows = jnp.concatenate([right, x, left], axis=1).astype(BF16)
            wide[t] = dot(rows, spread).astype(BF16)

    kernel_in = w_in_ref[...]

    def first(t, carry):
        valid_t = block_i * TB - 2 + t >= 0
        for hh in range(HB + 2):
            lhs = jnp.concatenate(
                [wide[t + dt, :, hh * 48: hh * 48 + 144] for dt in range(3)], axis=1
            )
            hidden = (dot(lhs, kernel_in) + b_in_ref[...]).astype(BF16)
            hidden_ref[t, hh] = hidden
            v = hidden.astype(F32)
            scale = lax.rsqrt(jnp.mean(v * v, axis=-1, keepdims=True) + 1e-06)
            valid = valid_t
            if hh == 0:
                valid = valid_t & (band_i > 0)
            if hh == HB + 1:
                valid = valid_t & (band_i < HBANDS - 1)
            z = v * scale * gain_ref[...]
            act = jnp.where(valid, 0.5 * z * (1.0 + jnp.tanh(0.5 * z)), 0.0)
            right, left = shifted(act)
            acts[t, hh, :, :mid] = right.astype(BF16)
            acts[t, hh, :, mid: 2 * mid] = act.astype(BF16)
            acts[t, hh, :, 2 * mid:] = left.astype(BF16)
        return carry

    lax.fori_loop(0, frames, first, 0)
    for copy in copies:
        copy.wait()
    rows = HB * W
    for f in range(TB):
        acc[:, f * mid: (f + 1) * mid] = (
            hidden_ref[f + 2, 1: HB + 1].reshape(rows, mid).astype(F32) + b_mid_ref[...]
        )

    def second(dh, carry):
        def lhs(frame):
            return acts[frame, pl.ds(dh, HB)].reshape(rows, 3 * mid)

        acc[...] += dot(lhs(1), wcat[0, dh]) + dot(lhs(2), wcat[1, dh])
        acc[:, :mid] += dot(lhs(0), wcat[0, dh, :, mid:])
        acc[:, mid:] += dot(lhs(3), wcat[1, dh, :, :mid])
        return carry

    lax.fori_loop(0, 3, second, 0)
    for f in range(TB):
        out_ref[0, f] = acc[:, f * mid: (f + 1) * mid].astype(BF16).reshape(HB, W, mid)


def shards(latents, row_cell, w_in, b_in, gain, w_mid, b_mid):
    n = lax.axis_size("sp")
    near = gathered(latents, row_cell)
    mid = b_in.shape[0]
    vmem = pl.BlockSpec(memory_space=pltpu.VMEM)
    return pl.pallas_call(
        functools.partial(conv_kernel, n, near.shape[0] // 3),
        out_shape=jax.ShapeDtypeStruct((1, TB, HB, W, mid), BF16),
        in_specs=[vmem] * 5 + [pl.BlockSpec(memory_space=pl.ANY)],
        out_specs=vmem,
        scratch_shapes=[
            pltpu.VMEM((TB + 4, W, 384), BF16),
            pltpu.VMEM((TB + 2, HB + 2, W, 3 * mid), BF16),
            pltpu.VMEM((2, 3, 3 * mid, 2 * mid), BF16),
            pltpu.VMEM((TB + 2, HB + 2, W, mid), BF16),
            pltpu.VMEM((HB * W, TB * mid), F32),
            pltpu.SemaphoreType.DMA((4,)),
        ],
        compiler_params=pltpu.CompilerParams(vmem_limit_bytes=60 * 2**20),
        name="conv_block",
    )(
        near, w_in.reshape(27 * C_LAT, mid), b_in.reshape(1, mid), gain.reshape(1, mid),
        b_mid.reshape(1, mid), w_mid.reshape(3, 3, 3 * mid, mid),
    )


def solution(mesh):
    return jax.shard_map(
        shards,
        mesh=mesh,
        in_specs=(P(("grp", "sp"), None), P(("grp", "sp")), P(), P(), P(), P(), P()),
        out_specs=P(("grp", "sp"), None, None, None, None),
        check_vma=False,
    )
```

```python
import functools

import jax
import jax.numpy as jnp
from jax import lax
from jax.experimental import pallas as pl
from jax.experimental.pallas import tpu as pltpu
from jax.sharding import PartitionSpec as P

C_LAT = 16
W = 160
TB = 2
HBANDS = 8
HB = 4
HALF_ROWS = HB // 2
HALF_W = W // 2
OFFSET_TILES = 2 * HBANDS + HBANDS // 2
F32 = jnp.float32
BF16 = jnp.bfloat16


def iota(shape, dim):
    return lax.broadcasted_iota(jnp.int32, shape, dim)


def dot(a, b, dims=((1,), (0,))):
    return lax.dot_general(a, b, (dims, ((), ())), preferred_element_type=F32)


def gather_kernel(n, slots, depth, lat_ref, cell_ref, out_ref, pack, arrived, mine, near,
                  send_a, recv_a, send_b, recv_b):
    me = lax.axis_index("sp")
    toks = lat_ref.shape[1]
    barrier = pltpu.get_barrier_semaphore()
    for delta in range(1, n):
        pl.semaphore_signal(
            barrier, inc=1, device_id={"sp": lax.rem(me + delta, n)},
            device_id_type=pl.DeviceIdType.MESH,
        )
    cell = cell_ref[...].reshape(1, toks).astype(F32)
    line = jnp.floor((cell + 0.5) * (1.0 / HALF_W))
    column = cell - HALF_W * line
    token_rows = HALF_ROWS * HBANDS
    frame = jnp.floor((line + 0.5) * (1.0 / token_rows))
    token_row = line - token_rows * frame
    time_block = jnp.floor((frame + 0.5) * (1.0 / TB))
    band = jnp.floor((token_row + 0.5) * (1.0 / HALF_ROWS))
    place_row = (frame - TB * time_block) * HALF_ROWS + token_row - HALF_ROWS * band
    owner = time_block * HBANDS + band - (OFFSET_TILES % n)
    owner = jnp.where(owner < 0, owner + n, owner)
    hits = owner == iota((n, toks), 0).astype(F32)
    hits = jnp.where(hits, 1.0, 0.0)
    before = jnp.where(iota((toks, toks), 0) < iota((toks, toks), 1), 1.0, 0.0).astype(BF16)
    ranks = dot(hits.astype(BF16), before)
    rank = jnp.sum(ranks * hits, axis=0, keepdims=True)
    target = owner * slots + rank
    picks = jnp.where(target == iota((n * slots, toks), 0).astype(F32), 1.0, 0.0).astype(BF16)
    which = iota((64, toks), 0)
    places = jnp.where(which == 0, place_row + 1.0, jnp.where(which == 1, column, 0.0)).astype(BF16)
    packed = jnp.concatenate([lat_ref[...], places], axis=0)
    packed = dot(picks, packed, ((1,), (1,))).astype(BF16)
    pack[...] = packed.reshape(n, slots, 128)
    arrived[pl.ds(me, 1)] = pack[pl.ds(me, 1)]
    pl.semaphore_wait(barrier, n - 1)
    copies = []
    for delta in range(1, n):
        to = lax.rem(me + delta, n)
        copy = pltpu.make_async_remote_copy(
            src_ref=pack.at[to], dst_ref=arrived.at[me],
            send_sem=send_a.at[delta - 1], recv_sem=recv_a.at[delta - 1],
            device_id={"sp": to}, device_id_type=pl.DeviceIdType.MESH,
        )
        copy.start()
        copies.append(copy)
    for copy in copies:
        copy.wait()
    got = arrived[...].reshape(n * slots, 128)
    got32 = got.astype(F32)
    ident = (got32[:, 64:65] - 1.0) * HALF_W + got32[:, 65:66]
    tokens = got[:, :64]
    odd = (iota((C_LAT, W), 1) & 1) == 1
    half = (iota((1, W), 1) >> 1).astype(F32)
    pieces = []
    for line_in in range(TB * HALF_ROWS):
        spots = jnp.where(ident == half + float(line_in * HALF_W), 1.0, 0.0).astype(BF16)
        grid = dot(tokens, spots, ((0,), (0,)))
        for a in range(2):
            base = a * 2 * C_LAT
            pieces.append(
                jnp.where(odd, grid[base + C_LAT: base + 2 * C_LAT], grid[base: base + C_LAT])
            )
    tile = jnp.concatenate(pieces, axis=0).T.astype(BF16)
    mine[...] = tile

    e = lax.rem(me + OFFSET_TILES, n)
    band_i = lax.rem(e, HBANDS)
    block_i = e // HBANDS
    blocks = n // HBANDS
    for phase in range(3):
        for k in range(depth):
            for side in range(3):
                if k == 0 and side == 1:
                    if phase == 0:
                        out_ref[1] = tile
                    continue
                slot = k * 3 + side
                shift = side - 1
                reader = lax.rem(me + k * HBANDS - shift + n, n)
                send_ok = (block_i + k < blocks)
                if shift == 1:
                    send_ok &= band_i > 0
                if shift == -1:
                    send_ok &= band_i < HBANDS - 1
                recv_ok = block_i >= k
                if shift == 1:
                    recv_ok &= band_i < HBANDS - 1
                if shift == -1:
                    recv_ok &= band_i > 0
                copy = pltpu.make_async_remote_copy(
                    src_ref=mine, dst_ref=near.at[slot],
                    send_sem=send_b.at[slot], recv_sem=recv_b.at[slot],
                    device_id={"sp": reader}, device_id_type=pl.DeviceIdType.MESH,
                )
                if phase == 0:
                    pl.when(send_ok)(copy.start)
                elif phase == 1:
                    def take():
                        copy.wait_recv()
                        out_ref[slot] = near[slot]

                    def blank():
                        out_ref[slot] = jnp.zeros_like(tile)

                    pl.when(recv_ok)(take)
                    pl.when(jnp.logical_not(recv_ok))(blank)
                else:
                    pl.when(send_ok)(copy.wait_send)


def gathered(latents, row_cell):
    n = lax.axis_size("sp")
    toks = latents.shape[0]
    slots = -(-2 * (toks // n) // 16) * 16
    depth = min(3, n // HBANDS)
    return pl.pallas_call(
        functools.partial(gather_kernel, n, slots, depth),
        out_shape=jax.ShapeDtypeStruct((depth * 3, W, 128), BF16),
        in_specs=[pl.BlockSpec(memory_space=pltpu.VMEM)] * 2,
        out_specs=pl.BlockSpec(memory_space=pltpu.VMEM),
        scratch_shapes=[
            pltpu.VMEM((n, slots, 128), BF16),
            pltpu.VMEM((n, slots, 128), BF16),
            pltpu.VMEM((W, 128), BF16),
            pltpu.VMEM((depth * 3, W, 128), BF16),
            pltpu.SemaphoreType.DMA((n - 1,)),
            pltpu.SemaphoreType.DMA((n - 1,)),
            pltpu.SemaphoreType.DMA((depth * 3,)),
            pltpu.SemaphoreType.DMA((depth * 3,)),
        ],
        compiler_params=pltpu.CompilerParams(collective_id=0, has_side_effects=True),
        name="gather_tiles",
    )(latents.T, row_cell)


def shifted(x):
    where = iota(x.shape, 0)
    right = jnp.where(where == 0, 0.0, pltpu.roll(x, 1, 0))
    left = jnp.where(where == W - 1, 0.0, pltpu.roll(x, W - 1, 0))
    return right, left


def conv_kernel(n, depth, near_ref, w_in_ref, b_in_ref, gain_ref, b_mid_ref, w_mid_ref, out_ref,
                wide, acts, wcat, hidden_ref, acc, sems):
    mid = b_in_ref.shape[0]
    b_in, gain, b_mid = [ref[...].reshape(1, mid) for ref in (b_in_ref, gain_ref, b_mid_ref)]
    frames = TB + 2
    copies = []
    for index, (half, position, tap) in enumerate(((0, 1, 0), (0, 0, 1), (1, 1, 1), (1, 0, 2))):
        copy = pltpu.make_async_copy(
            w_mid_ref.at[tap], wcat.at[half, :, :, pl.ds(position * mid, mid)], sems.at[index]
        )
        copy.start()
        copies.append(copy)
    e = lax.rem(lax.axis_index("sp") + OFFSET_TILES, n)
    band_i = lax.rem(e, HBANDS)
    block_i = e // HBANDS
    lane = iota((W, 128), 1)
    source = iota((384, 1), 0)
    spread_to = ((source >> 4) & 7) * 48 + (source >> 7) * 16 + (source & 15)
    spread = jnp.where(spread_to == iota((384, 384), 1), 1.0, 0.0).astype(BF16)
    for k in range(3):
        for f in range(TB):
            t = (2 - k) * TB + f
            if k >= depth:
                wide[t] = jnp.zeros((W, 384), BF16)
                continue
            up, own, down = [near_ref[3 * k + side].astype(F32) for side in range(3)]
            x = jnp.where(
                lane < 32, pltpu.roll(up, 96 - 64 * f, 1),
                jnp.where(lane < 96, pltpu.roll(own, (32 - 64 * f) % 128, 1),
                          pltpu.roll(down, (96 - 64 * f) % 128, 1)),
            )
            right, left = shifted(x)
            rows = jnp.concatenate([right, x, left], axis=1).astype(BF16)
            wide[t] = dot(rows, spread).astype(BF16)

    kernel_in = w_in_ref[...]

    def first(t, carry):
        valid_t = block_i * TB - 2 + t >= 0
        for hh in range(HB + 2):
            lhs = jnp.concatenate(
                [wide[t + dt, :, hh * 48: hh * 48 + 144] for dt in range(3)], axis=1
            )
            hidden = (dot(lhs, kernel_in) + b_in).astype(BF16)
            hidden_ref[t, hh] = hidden
            v = hidden.astype(F32)
            scale = lax.rsqrt(jnp.mean(v * v, axis=-1, keepdims=True) + 1e-06)
            valid = valid_t
            if hh == 0:
                valid = valid_t & (band_i > 0)
            if hh == HB + 1:
                valid = valid_t & (band_i < HBANDS - 1)
            z = v * scale * gain
            act = jnp.where(valid, 0.5 * z * (1.0 + jnp.tanh(0.5 * z)), 0.0)
            right, left = shifted(act)
            acts[t, hh, :, :mid] = right.astype(BF16)
            acts[t, hh, :, mid: 2 * mid] = act.astype(BF16)
            acts[t, hh, :, 2 * mid:] = left.astype(BF16)
        return carry

    lax.fori_loop(0, frames, first, 0)
    for copy in copies:
        copy.wait()
    rows = HB * W
    for f in range(TB):
        acc[:, f * mid: (f + 1) * mid] = (
            hidden_ref[f + 2, 1: HB + 1].reshape(rows, mid).astype(F32) + b_mid
        )

    def second(dh, carry):
        def lhs(frame):
            return acts[frame, pl.ds(dh, HB)].reshape(rows, 3 * mid)

        acc[...] += dot(lhs(1), wcat[0, dh]) + dot(lhs(2), wcat[1, dh])
        acc[:, :mid] += dot(lhs(0), wcat[0, dh, :, mid:])
        acc[:, mid:] += dot(lhs(3), wcat[1, dh, :, :mid])
        return carry

    lax.fori_loop(0, 3, second, 0)
    for f in range(TB):
        out_ref[0, f] = acc[:, f * mid: (f + 1) * mid].astype(BF16).reshape(HB, W, mid)


def shards(latents, row_cell, w_in, b_in, gain, w_mid, b_mid):
    n = lax.axis_size("sp")
    near = gathered(latents, row_cell)
    mid = b_in.shape[0]
    vmem = pl.BlockSpec(memory_space=pltpu.VMEM)
    return pl.pallas_call(
        functools.partial(conv_kernel, n, near.shape[0] // 3),
        out_shape=jax.ShapeDtypeStruct((1, TB, HB, W, mid), BF16),
        in_specs=[vmem] * 5 + [pl.BlockSpec(memory_space=pl.ANY)],
        out_specs=vmem,
        scratch_shapes=[
            pltpu.VMEM((TB + 4, W, 384), BF16),
            pltpu.VMEM((TB + 2, HB + 2, W, 3 * mid), BF16),
            pltpu.VMEM((2, 3, 3 * mid, 2 * mid), BF16),
            pltpu.VMEM((TB + 2, HB + 2, W, mid), BF16),
            pltpu.VMEM((HB * W, TB * mid), F32),
            pltpu.SemaphoreType.DMA((4,)),
        ],
        compiler_params=pltpu.CompilerParams(vmem_limit_bytes=60 * 2**20),
        name="conv_block",
    )(
        near, w_in.reshape(27 * C_LAT, mid), b_in, gain, b_mid, w_mid.reshape(3, 3, 3 * mid, mid),
    )


def solution(mesh):
    return jax.shard_map(
        shards,
        mesh=mesh,
        in_specs=(P(("grp", "sp"), None), P(("grp", "sp")), P(), P(), P(), P(), P()),
        out_specs=P(("grp", "sp"), None, None, None, None),
        check_vma=False,
    )
```

```python
import functools

import jax
import jax.numpy as jnp
from jax import lax
from jax.experimental import pallas as pl
from jax.experimental.pallas import tpu as pltpu
from jax.sharding import PartitionSpec as P

C_LAT = 16
W = 160
TB = 2
HBANDS = 8
HB = 4
HALF_ROWS = HB // 2
HALF_W = W // 2
OFFSET_TILES = 2 * HBANDS + HBANDS // 2
F32 = jnp.float32
BF16 = jnp.bfloat16


def iota(shape, dim):
    return lax.broadcasted_iota(jnp.int32, shape, dim)


def dot(a, b, dims=((1,), (0,))):
    return lax.dot_general(a, b, (dims, ((), ())), preferred_element_type=F32)


def gather_kernel(n, slots, depth, lat_ref, cell_ref, out_ref, pack, arrived, mine, near,
                  send_a, recv_a, send_b, recv_b):
    me = lax.axis_index("sp")
    toks = lat_ref.shape[1]
    barrier = pltpu.get_barrier_semaphore()
    for delta in range(1, n):
        pl.semaphore_signal(
            barrier, inc=1, device_id={"sp": lax.rem(me + delta, n)},
            device_id_type=pl.DeviceIdType.MESH,
        )
    cell = cell_ref[...].reshape(1, toks).astype(F32)
    line = jnp.floor((cell + 0.5) * (1.0 / HALF_W))
    column = cell - HALF_W * line
    token_rows = HALF_ROWS * HBANDS
    frame = jnp.floor((line + 0.5) * (1.0 / token_rows))
    token_row = line - token_rows * frame
    time_block = jnp.floor((frame + 0.5) * (1.0 / TB))
    band = jnp.floor((token_row + 0.5) * (1.0 / HALF_ROWS))
    place_row = (frame - TB * time_block) * HALF_ROWS + token_row - HALF_ROWS * band
    owner = time_block * HBANDS + band - (OFFSET_TILES % n)
    owner = jnp.where(owner < 0, owner + n, owner)
    hits = owner == iota((n, toks), 0).astype(F32)
    hits = jnp.where(hits, 1.0, 0.0)
    before = jnp.where(iota((toks, toks), 0) < iota((toks, toks), 1), 1.0, 0.0).astype(BF16)
    ranks = dot(hits.astype(BF16), before)
    rank = jnp.sum(ranks * hits, axis=0, keepdims=True)
    target = owner * slots + rank
    picks = jnp.where(target == iota((n * slots, toks), 0).astype(F32), 1.0, 0.0).astype(BF16)
    which = iota((64, toks), 0)
    places = jnp.where(which == 0, place_row + 1.0, jnp.where(which == 1, column, 0.0)).astype(BF16)
    packed = jnp.concatenate([lat_ref[...], places], axis=0)
    packed = dot(picks, packed, ((1,), (1,))).astype(BF16)
    pack[...] = packed.reshape(n, slots, 128)
    arrived[pl.ds(me, 1)] = pack[pl.ds(me, 1)]
    pl.semaphore_wait(barrier, n - 1)
    copies = []
    for delta in range(1, n):
        to = lax.rem(me + delta, n)
        copy = pltpu.make_async_remote_copy(
            src_ref=pack.at[to], dst_ref=arrived.at[me],
            send_sem=send_a.at[delta - 1], recv_sem=recv_a.at[delta - 1],
            device_id={"sp": to}, device_id_type=pl.DeviceIdType.MESH,
        )
        copy.start()
        copies.append(copy)
    for copy in copies:
        copy.wait()
    got = arrived[...].reshape(n * slots, 128)
    got32 = got.astype(F32)
    ident = (got32[:, 64:65] - 1.0) * HALF_W + got32[:, 65:66]
    tokens = got[:, :64]
    odd = (iota((C_LAT, W), 1) & 1) == 1
    half = (iota((1, W), 1) >> 1).astype(F32)
    pieces = []
    for line_in in range(TB * HALF_ROWS):
        spots = jnp.where(ident == half + float(line_in * HALF_W), 1.0, 0.0).astype(BF16)
        grid = dot(tokens, spots, ((0,), (0,)))
        for a in range(2):
            base = a * 2 * C_LAT
            pieces.append(
                jnp.where(odd, grid[base + C_LAT: base + 2 * C_LAT], grid[base: base + C_LAT])
            )
    tile = jnp.concatenate(pieces, axis=0).T.astype(BF16)
    mine[...] = tile

    e = lax.rem(me + OFFSET_TILES, n)
    band_i = lax.rem(e, HBANDS)
    block_i = e // HBANDS
    blocks = n // HBANDS
    for phase in range(3):
        for k in range(depth):
            for side in range(3):
                if k == 0 and side == 1:
                    if phase == 0:
                        out_ref[1] = tile
                    continue
                slot = k * 3 + side
                shift = side - 1
                reader = lax.rem(me + k * HBANDS - shift + n, n)
                send_ok = (block_i + k < blocks)
                if shift == 1:
                    send_ok &= band_i > 0
                if shift == -1:
                    send_ok &= band_i < HBANDS - 1
                recv_ok = block_i >= k
                if shift == 1:
                    recv_ok &= band_i < HBANDS - 1
                if shift == -1:
                    recv_ok &= band_i > 0
                copy = pltpu.make_async_remote_copy(
                    src_ref=mine, dst_ref=near.at[slot],
                    send_sem=send_b.at[slot], recv_sem=recv_b.at[slot],
                    device_id={"sp": reader}, device_id_type=pl.DeviceIdType.MESH,
                )
                if phase == 0:
                    pl.when(send_ok)(copy.start)
                elif phase == 1:
                    def take():
                        copy.wait_recv()
                        out_ref[slot] = near[slot]

                    def blank():
                        out_ref[slot] = jnp.zeros_like(tile)

                    pl.when(recv_ok)(take)
                    pl.when(jnp.logical_not(recv_ok))(blank)
                else:
                    pl.when(send_ok)(copy.wait_send)


def gathered(latents, row_cell):
    n = lax.axis_size("sp")
    toks = latents.shape[0]
    slots = -(-2 * (toks // n) // 16) * 16
    depth = min(3, n // HBANDS)
    return pl.pallas_call(
        functools.partial(gather_kernel, n, slots, depth),
        out_shape=jax.ShapeDtypeStruct((depth * 3, W, 128), BF16),
        in_specs=[pl.BlockSpec(memory_space=pltpu.VMEM)] * 2,
        out_specs=pl.BlockSpec(memory_space=pltpu.VMEM),
        scratch_shapes=[
            pltpu.VMEM((n, slots, 128), BF16),
            pltpu.VMEM((n, slots, 128), BF16),
            pltpu.VMEM((W, 128), BF16),
            pltpu.VMEM((depth * 3, W, 128), BF16),
            pltpu.SemaphoreType.DMA((n - 1,)),
            pltpu.SemaphoreType.DMA((n - 1,)),
            pltpu.SemaphoreType.DMA((depth * 3,)),
            pltpu.SemaphoreType.DMA((depth * 3,)),
        ],
        compiler_params=pltpu.CompilerParams(collective_id=0, has_side_effects=True),
        name="gather_tiles",
    )(latents.T, row_cell)


def shifted(x):
    where = iota(x.shape, 0)
    right = jnp.where(where == 0, 0.0, pltpu.roll(x, 1, 0))
    left = jnp.where(where == W - 1, 0.0, pltpu.roll(x, W - 1, 0))
    return right, left


def conv_kernel(n, depth, near_ref, w_in_ref, b_in_ref, gain_ref, b_mid_ref, w_mid_ref, out_ref,
                wide, taps_in, scales, acts, wcat, hidden_ref, sems):
    mid = b_in_ref.shape[0]
    b_in, gain, b_mid = [ref[...].reshape(1, mid) for ref in (b_in_ref, gain_ref, b_mid_ref)]
    frames = TB + 2
    copies = []
    for index, (half, position, tap) in enumerate(((0, 1, 0), (0, 0, 1), (1, 1, 1), (1, 0, 2))):
        copy = pltpu.make_async_copy(
            w_mid_ref.at[tap], wcat.at[half, :, :, pl.ds(position * mid, mid)], sems.at[index]
        )
        copy.start()
        copies.append(copy)
    e = lax.rem(lax.axis_index("sp") + OFFSET_TILES, n)
    band_i = lax.rem(e, HBANDS)
    block_i = e // HBANDS
    lane = iota((W, 128), 1)
    source = iota((384, 1), 0)
    spread_to = ((source >> 4) & 7) * 64 + (source >> 7) * 16 + (source & 15)
    spread = jnp.where(spread_to == iota((384, 512), 1), 1.0, 0.0).astype(BF16)
    for k in range(3):
        for f in range(TB):
            t = (2 - k) * TB + f
            if k >= depth:
                wide[t] = jnp.zeros((2, W, 512), BF16)
                continue
            up, own, down = [near_ref[3 * k + side].astype(F32) for side in range(3)]
            x = jnp.where(
                lane < 32, pltpu.roll(up, 96 - 64 * f, 1),
                jnp.where(lane < 96, pltpu.roll(own, (32 - 64 * f) % 128, 1),
                          pltpu.roll(down, (96 - 64 * f) % 128, 1)),
            )
            right, left = shifted(x)
            rows = jnp.concatenate([right, x, left], axis=1).astype(BF16)
            lines = dot(rows, spread)
            wide[t, 0] = lines.astype(BF16)
            wide[t, 1] = pltpu.roll(lines, 448, 1).astype(BF16)

    taps_in[...] = jnp.zeros_like(taps_in)
    for dt in range(3):
        for dh in range(3):
            base = (dt * 3 + dh) * 48
            taps_in[dt, dh * 64: dh * 64 + 48] = w_in_ref[base: base + 48]

    half_gain = 0.5 * gain
    pairs = (HB + 2) // 2
    steps = frames * pairs

    def convolve(step):
        t = step // pairs
        pair = lax.rem(step, pairs)
        lanes = pl.ds(pl.multiple_of(pair * 128, 128), 256)
        lhs = jnp.concatenate(
            [wide[t + dt, :, :, lanes].reshape(2 * W, 256) for dt in range(3)], axis=1
        )
        hidden = (dot(lhs, taps_in[...].reshape(768, mid)) + b_in).astype(BF16)
        hidden_ref[t, pl.ds(2 * pair, 2)] = hidden.reshape(2, W, mid)
        v = hidden.astype(F32)
        scale = lax.rsqrt(jnp.mean(v * v, axis=-1, keepdims=True) + 1e-06)
        scales[...] = jnp.broadcast_to(scale, scales.shape)

    def activate(step):
        t = step // pairs
        pair = lax.rem(step, pairs)
        valid_t = block_i * TB - 2 + t >= 0
        for side in range(2):
            hh = 2 * pair + side
            v = hidden_ref[t, hh].astype(F32)
            if side == 0:
                valid = valid_t & ((band_i > 0) | (pair > 0))
            else:
                valid = valid_t & ((band_i < HBANDS - 1) | (pair < pairs - 1))
            scale = jnp.where(valid, scales[side * W: (side + 1) * W, :1], 0.0)
            z = v * scale * half_gain
            act = z + z * jnp.tanh(z)
            zero = jnp.zeros((1, mid), F32)
            right = jnp.concatenate([zero, act[:-1]], axis=0)
            left = jnp.concatenate([act[1:], zero], axis=0)
            acts[t, hh, :, :mid] = right.astype(BF16)
            acts[t, hh, :, mid: 2 * mid] = act.astype(BF16)
            acts[t, hh, :, 2 * mid:] = left.astype(BF16)

    convolve(0)

    def first(step, carry):
        activate(step - 1)
        convolve(step)
        return carry

    lax.fori_loop(1, steps, first, 0)
    activate(steps - 1)
    for copy in copies:
        copy.wait()
    rows = HB * W

    def lhs(frame):
        return jnp.concatenate(
            [acts[frame, dh: dh + HB].reshape(rows, 3 * mid) for dh in range(3)], axis=1
        )

    def tap(half, lanes):
        return wcat[half, :, :, lanes].reshape(9 * mid, -1)

    both = slice(0, 2 * mid)
    mixed = dot(lhs(1), tap(0, both)) + dot(lhs(2), tap(1, both))
    edges = (dot(lhs(0), tap(0, slice(mid, 2 * mid))), dot(lhs(3), tap(1, slice(0, mid))))
    for f in range(TB):
        total = mixed[:, f * mid: (f + 1) * mid] + edges[f] + b_mid
        total += hidden_ref[f + 2, 1: HB + 1].reshape(rows, mid).astype(F32)
        out_ref[0, f] = total.astype(BF16).reshape(HB, W, mid)


def shards(latents, row_cell, w_in, b_in, gain, w_mid, b_mid):
    n = lax.axis_size("sp")
    near = gathered(latents, row_cell)
    mid = b_in.shape[0]
    vmem = pl.BlockSpec(memory_space=pltpu.VMEM)
    return pl.pallas_call(
        functools.partial(conv_kernel, n, near.shape[0] // 3),
        out_shape=jax.ShapeDtypeStruct((1, TB, HB, W, mid), BF16),
        in_specs=[vmem] * 5 + [pl.BlockSpec(memory_space=pl.ANY)],
        out_specs=vmem,
        scratch_shapes=[
            pltpu.VMEM((TB + 4, 2, W, 512), BF16),
            pltpu.VMEM((3, 256, mid), BF16),
            pltpu.VMEM((2 * W, 128), F32),
            pltpu.VMEM((TB + 2, HB + 2, W, 3 * mid), BF16),
            pltpu.VMEM((2, 3, 3 * mid, 2 * mid), BF16),
            pltpu.VMEM((TB + 2, HB + 2, W, mid), BF16),
            pltpu.SemaphoreType.DMA((4,)),
        ],
        compiler_params=pltpu.CompilerParams(vmem_limit_bytes=60 * 2**20),
        name="conv_block",
    )(
        near, w_in.reshape(27 * C_LAT, mid), b_in, gain, b_mid, w_mid.reshape(3, 3, 3 * mid, mid),
    )


def solution(mesh):
    return jax.shard_map(
        shards,
        mesh=mesh,
        in_specs=(P(("grp", "sp"), None), P(("grp", "sp")), P(), P(), P(), P(), P()),
        out_specs=P(("grp", "sp"), None, None, None, None),
        check_vma=False,
    )
```

```python
import functools

import jax
import jax.numpy as jnp
from jax import lax
from jax.experimental import pallas as pl
from jax.experimental.pallas import tpu as pltpu
from jax.sharding import PartitionSpec as P

C_LAT = 16
W = 160
TB = 2
HBANDS = 8
HB = 4
HALF_ROWS = HB // 2
HALF_W = W // 2
OFFSET_TILES = 2 * HBANDS + HBANDS // 2
F32 = jnp.float32
BF16 = jnp.bfloat16


def iota(shape, dim):
    return lax.broadcasted_iota(jnp.int32, shape, dim)


def dot(a, b, dims=((1,), (0,))):
    return lax.dot_general(a, b, (dims, ((), ())), preferred_element_type=F32)


def gather_kernel(n, per, height, depth, lat_ref, cell_ref, out_ref, pack, arrived, mine, above,
                  below, near,
                  send_a, recv_a, send_b, recv_b):
    me = lax.axis_index("sp")
    toks = lat_ref.shape[1]
    barrier = pltpu.get_barrier_semaphore()
    for delta in range(1, n):
        pl.semaphore_signal(
            barrier, inc=1, device_id={"sp": lax.rem(me + delta, n)},
            device_id_type=pl.DeviceIdType.MESH,
        )
    cell = cell_ref[...].reshape(1, toks).astype(F32)
    line = jnp.floor((cell + 0.5) * (1.0 / HALF_W))
    column = cell - HALF_W * line
    token_rows = HALF_ROWS * HBANDS
    frame = jnp.floor((line + 0.5) * (1.0 / token_rows))
    token_row = line - token_rows * frame
    time_block = jnp.floor((frame + 0.5) * (1.0 / TB))
    band = jnp.floor((token_row + 0.5) * (1.0 / HALF_ROWS))
    place_row = (frame - TB * time_block) * HALF_ROWS + token_row - HALF_ROWS * band
    owner = time_block * HBANDS + band - (OFFSET_TILES % n)
    owner = jnp.where(owner < 0, owner + n, owner)
    hits = owner == iota((n, toks), 0).astype(F32)
    hits = jnp.where(hits, 1.0, 0.0)
    before = jnp.where(iota((toks, toks), 0) < iota((toks, toks), 1), 1.0, 0.0).astype(BF16)
    ranks = dot(hits.astype(BF16), before)
    rank = jnp.sum(ranks * hits, axis=0, keepdims=True)
    dest = iota((n, height, toks), 0).astype(F32)
    row = iota((n, height, toks), 1).astype(F32)
    hit = owner.reshape(1, 1, toks) == dest
    rank3 = rank.reshape(1, 1, toks)

    def block(value):
        return value.reshape(n * height, toks).astype(BF16)

    low = block(jnp.where(hit & (rank3 == row) & (row < per), 1.0, 0.0))
    high = block(jnp.where(hit & (rank3 == row + per) & (row < per), 1.0, 0.0))
    notes = jnp.where(row == per, place_row.reshape(1, 1, toks) + 1.0,
                      jnp.where(row == per + 1, column.reshape(1, 1, toks), 0.0))
    notes = block(jnp.where(hit, notes, 0.0))
    lane_of = jnp.where(rank < per, rank, rank + float(height - per))
    lanes = jnp.where(lane_of == iota((128, toks), 0).astype(F32), 1.0, 0.0).astype(BF16)
    nt = ((1,), (1,))
    packed = jnp.concatenate(
        [dot(low, lat_ref[...], nt), dot(high, lat_ref[...], nt)], axis=1
    ) + dot(notes, lanes, nt)
    pack[...] = packed.reshape(n, height, 128).astype(BF16)
    arrived[pl.ds(me, 1)] = pack[pl.ds(me, 1)]
    pl.semaphore_wait(barrier, n - 1)
    copies = []
    for delta in range(1, n):
        to = lax.rem(me + delta, n)
        copy = pltpu.make_async_remote_copy(
            src_ref=pack.at[to], dst_ref=arrived.at[me],
            send_sem=send_a.at[delta - 1], recv_sem=recv_a.at[delta - 1],
            device_id={"sp": to}, device_id_type=pl.DeviceIdType.MESH,
        )
        copy.start()
        copies.append(copy)
    for copy in copies:
        copy.wait()
    got3 = arrived[...].astype(F32)
    got = got3.reshape(n * height, 128).astype(BF16)
    unit = jnp.where(iota((2 * height, 128), 0) == iota((2 * height, 128), 1), 1.0, 0.0).astype(BF16)
    ident = (
        (dot(unit, got3[:, per].astype(BF16), nt) - 1.0) * HALF_W
        + dot(unit, got3[:, per + 1].astype(BF16), nt)
    )
    idents = [
        jnp.concatenate([ident[h * height: (h + 1) * height, s: s + 1] for s in range(n)], axis=0)
        for h in range(2)
    ]
    odd = (iota((C_LAT, W), 1) & 1) == 1
    half = (iota((1, W), 1) >> 1).astype(F32)
    pieces = []
    for line_in in range(TB * HALF_ROWS):
        grid = 0.0
        for h in range(2):
            spots = jnp.where(idents[h] == half + float(line_in * HALF_W), 1.0, 0.0).astype(BF16)
            grid += dot(got[:, 64 * h: 64 * h + 64], spots, ((0,), (0,)))
        for a in range(2):
            base = a * 2 * C_LAT
            pieces.append(
                jnp.where(odd, grid[base + C_LAT: base + 2 * C_LAT], grid[base: base + C_LAT])
            )
    tile = jnp.concatenate(pieces, axis=0).T.astype(BF16)
    mine[...] = tile
    for edge, top in ((above, HB - 2), (below, 0)):
        rim = jnp.concatenate([pieces[f * HB + top + r] for f in range(TB) for r in range(2)], axis=0)
        edge[...] = jnp.concatenate([rim[:, :HALF_W], rim[:, HALF_W:]], axis=0).T.astype(BF16)

    e = lax.rem(me + OFFSET_TILES, n)
    band_i = lax.rem(e, HBANDS)
    block_i = e // HBANDS
    blocks = n // HBANDS
    for phase in range(3):
        for k in range(depth):
            for side in range(3):
                if k == 0 and side == 1:
                    if phase == 0:
                        out_ref[0, :W] = tile
                    continue
                slot = k * 3 + side
                start, size = ((W, HALF_W), (0, W), (W + HALF_W, HALF_W))[side]
                part = pl.ds(start, size)
                shift = side - 1
                reader = lax.rem(me + k * HBANDS - shift + n, n)
                send_ok = (block_i + k < blocks)
                if shift == 1:
                    send_ok &= band_i > 0
                if shift == -1:
                    send_ok &= band_i < HBANDS - 1
                recv_ok = block_i >= k
                if shift == 1:
                    recv_ok &= band_i < HBANDS - 1
                if shift == -1:
                    recv_ok &= band_i > 0
                copy = pltpu.make_async_remote_copy(
                    src_ref=(above, mine, below)[side], dst_ref=near.at[k, part],
                    send_sem=send_b.at[slot], recv_sem=recv_b.at[slot],
                    device_id={"sp": reader}, device_id_type=pl.DeviceIdType.MESH,
                )
                if phase == 0:
                    pl.when(send_ok)(copy.start)
                elif phase == 1:
                    def take():
                        copy.wait_recv()
                        out_ref[k, part] = near[k, part]

                    def blank():
                        out_ref[k, part] = jnp.zeros((size, 128), BF16)

                    pl.when(recv_ok)(take)
                    pl.when(jnp.logical_not(recv_ok))(blank)
                else:
                    pl.when(send_ok)(copy.wait_send)


def gathered(latents, row_cell):
    n = lax.axis_size("sp")
    toks = latents.shape[0]
    per = toks // n
    height = -(-(per + 2) // 8) * 8
    depth = min(3, n // HBANDS)
    return pl.pallas_call(
        functools.partial(gather_kernel, n, per, height, depth),
        out_shape=jax.ShapeDtypeStruct((depth, 2 * W, 128), BF16),
        in_specs=[pl.BlockSpec(memory_space=pltpu.VMEM)] * 2,
        out_specs=pl.BlockSpec(memory_space=pltpu.VMEM),
        scratch_shapes=[
            pltpu.VMEM((n, height, 128), BF16),
            pltpu.VMEM((n, height, 128), BF16),
            pltpu.VMEM((W, 128), BF16),
            pltpu.VMEM((HALF_W, 128), BF16),
            pltpu.VMEM((HALF_W, 128), BF16),
            pltpu.VMEM((depth, 2 * W, 128), BF16),
            pltpu.SemaphoreType.DMA((n - 1,)),
            pltpu.SemaphoreType.DMA((n - 1,)),
            pltpu.SemaphoreType.DMA((depth * 3,)),
            pltpu.SemaphoreType.DMA((depth * 3,)),
        ],
        compiler_params=pltpu.CompilerParams(collective_id=0, has_side_effects=True),
        name="gather_tiles",
    )(latents.T, row_cell)


def shifted(x):
    where = iota(x.shape, 0)
    right = jnp.where(where == 0, 0.0, pltpu.roll(x, 1, 0))
    left = jnp.where(where == W - 1, 0.0, pltpu.roll(x, W - 1, 0))
    return right, left


def conv_kernel(n, depth, near_ref, w_in_ref, b_in_ref, gain_ref, b_mid_ref, w_mid_ref, out_ref,
                wide, acts, wcat, hidden_ref, sems):
    mid = b_in_ref.shape[0]
    b_in, gain, b_mid = [ref[...].reshape(1, mid) for ref in (b_in_ref, gain_ref, b_mid_ref)]
    frames = TB + 2
    copies = []
    for index, (half, position, tap) in enumerate(((0, 1, 0), (0, 0, 1), (1, 1, 1), (1, 0, 2))):
        copy = pltpu.make_async_copy(
            w_mid_ref.at[tap], wcat.at[half, :, :, pl.ds(position * mid, mid)], sems.at[index]
        )
        copy.start()
        copies.append(copy)
    e = lax.rem(lax.axis_index("sp") + OFFSET_TILES, n)
    band_i = lax.rem(e, HBANDS)
    block_i = e // HBANDS
    lane = iota((W, 128), 1)
    source = iota((384, 1), 0)
    spread_to = ((source >> 4) & 7) * 48 + (source >> 7) * 16 + (source & 15)
    spread = jnp.where(spread_to == iota((384, 384), 1), 1.0, 0.0).astype(BF16)
    for k in range(3):
        for f in range(TB):
            t = (2 - k) * TB + f
            if k >= depth:
                wide[t] = jnp.zeros((W, 384), BF16)
                continue
            own = near_ref[k, :W].astype(F32)
            up, down = [
                jnp.concatenate([pltpu.roll(rim, (to - 32 * f) % 128, 1),
                                 pltpu.roll(rim, (to - 64 - 32 * f) % 128, 1)], axis=0)
                for rim, to in ((near_ref[k, W: W + HALF_W].astype(F32), 0),
                                (near_ref[k, W + HALF_W:].astype(F32), 96))
            ]
            x = jnp.where(
                lane < 32, up,
                jnp.where(lane < 96, pltpu.roll(own, (32 - 64 * f) % 128, 1), down),
            )
            right, left = shifted(x)
            rows = jnp.concatenate([right, x, left], axis=1).astype(BF16)
            wide[t] = dot(rows, spread).astype(BF16)

    kernel_in = w_in_ref[...]

    def first(t, carry):
        valid_t = block_i * TB - 2 + t >= 0
        for hh in range(HB + 2):
            lhs = jnp.concatenate(
                [wide[t + dt, :, hh * 48: hh * 48 + 144] for dt in range(3)], axis=1
            )
            hidden = (dot(lhs, kernel_in) + b_in).astype(BF16)
            hidden_ref[t, hh] = hidden
            v = hidden.astype(F32)
            scale = lax.rsqrt(jnp.mean(v * v, axis=-1, keepdims=True) + 1e-06)
            valid = valid_t
            if hh == 0:
                valid = valid_t & (band_i > 0)
            if hh == HB + 1:
                valid = valid_t & (band_i < HBANDS - 1)
            z = v * scale * gain
            act = jnp.where(valid, 0.5 * z * (1.0 + jnp.tanh(0.5 * z)), 0.0)
            right, left = shifted(act)
            acts[t, hh, :, :mid] = right.astype(BF16)
            acts[t, hh, :, mid: 2 * mid] = act.astype(BF16)
            acts[t, hh, :, 2 * mid:] = left.astype(BF16)
        return carry

    lax.fori_loop(0, frames, first, 0)
    for copy in copies:
        copy.wait()
    rows = HB * W

    def lhs(frame):
        return jnp.concatenate(
            [acts[frame, dh: dh + HB].reshape(rows, 3 * mid) for dh in range(3)], axis=1
        )

    def tap(half, lanes):
        return wcat[half, :, :, lanes].reshape(9 * mid, -1)

    both = slice(0, 2 * mid)
    mixed = dot(lhs(1), tap(0, both)) + dot(lhs(2), tap(1, both))
    edges = (dot(lhs(0), tap(0, slice(mid, 2 * mid))), dot(lhs(3), tap(1, slice(0, mid))))
    for f in range(TB):
        total = mixed[:, f * mid: (f + 1) * mid] + edges[f] + b_mid
        total += hidden_ref[f + 2, 1: HB + 1].reshape(rows, mid).astype(F32)
        out_ref[0, f] = total.astype(BF16).reshape(HB, W, mid)


def shards(latents, row_cell, w_in, b_in, gain, w_mid, b_mid):
    n = lax.axis_size("sp")
    near = gathered(latents, row_cell)
    mid = b_in.shape[0]
    vmem = pl.BlockSpec(memory_space=pltpu.VMEM)
    return pl.pallas_call(
        functools.partial(conv_kernel, n, near.shape[0]),
        out_shape=jax.ShapeDtypeStruct((1, TB, HB, W, mid), BF16),
        in_specs=[vmem] * 5 + [pl.BlockSpec(memory_space=pl.ANY)],
        out_specs=vmem,
        scratch_shapes=[
            pltpu.VMEM((TB + 4, W, 384), BF16),
            pltpu.VMEM((TB + 2, HB + 2, W, 3 * mid), BF16),
            pltpu.VMEM((2, 3, 3 * mid, 2 * mid), BF16),
            pltpu.VMEM((TB + 2, HB + 2, W, mid), BF16),
            pltpu.SemaphoreType.DMA((4,)),
        ],
        compiler_params=pltpu.CompilerParams(vmem_limit_bytes=60 * 2**20),
        name="conv_block",
    )(
        near, w_in.reshape(27 * C_LAT, mid), b_in, gain, b_mid, w_mid.reshape(3, 3, 3 * mid, mid),
    )


def solution(mesh):
    return jax.shard_map(
        shards,
        mesh=mesh,
        in_specs=(P(("grp", "sp"), None), P(("grp", "sp")), P(), P(), P(), P(), P()),
        out_specs=P(("grp", "sp"), None, None, None, None),
        check_vma=False,
    )
```
